32 devices in a mesh: dp: 4 (over x, core), fsdp: 8 (over z, y).
Axes of the slice: x: 2, y: 2, z: 4, core: 2. Of those that a mesh axis runs over, the one named last changes fastest.
Arguments:
- hidden_in: bfloat16 [64, 512, 768], P(('dp', 'fsdp')), may hold values from -12 to 12
- prev_logits: bfloat16 [64, 12, 512, 512], P(('dp', 'fsdp')), may hold values from -6 to 6
- document: int32 [64, 512], P(('dp', 'fsdp')), may hold values from 0 to 512, as said below
- querymat: bfloat16 [768, 768], P(('dp', 'fsdp')), may hold values from -0.21875 to 0.21875
- querybias: bfloat16 [768], P(('dp', 'fsdp')), may hold values from -1.75 to 1.75
- keysmat: bfloat16 [768, 768], P(('dp', 'fsdp')), may hold values from -0.21875 to 0.21875
- valuemat: bfloat16 [768, 768], P(('dp', 'fsdp')), may hold values from -0.21875 to 0.21875
- valuebias: bfloat16 [768], P(('dp', 'fsdp')), may hold values from -1.75 to 1.75
- outputmat: bfloat16 [768, 768], P(('dp', 'fsdp')), may hold values from -0.875 to 0.875
- outputbias: bfloat16 [768], P(('dp', 'fsdp')), may hold values from -1.75 to 1.75
- normgain: bfloat16 [768], P(('dp', 'fsdp')), may hold values from 0.5 to 1.5
- normshift: bfloat16 [768], P(('dp', 'fsdp')), may hold values from -1.75 to 1.75
- innermat: bfloat16 [768, 3072], P(('dp', 'fsdp')), may hold values from -0.21875 to 0.21875
- innerbias: bfloat16 [3072], P(('dp', 'fsdp')), may hold values from -1.75 to 1.75
- outermat: bfloat16 [3072, 768], P(('dp', 'fsdp')), may hold values from -0.109375 to 0.109375
- outerbias: bfloat16 [768], P(('dp', 'fsdp')), may hold values from -1.75 to 1.75
- lastgain: bfloat16 [768], P(('dp', 'fsdp')), may hold values from 0.5 to 1.5
- lastshift: bfloat16 [768], P(('dp', 'fsdp')), may hold values from -1.75 to 1.75
- cotangent: bfloat16 [64, 512, 768], P(('dp', 'fsdp')), may hold values from -6 to 6
- logit_cotangent: bfloat16 [64, 12, 512, 512], P(('dp', 'fsdp')), may hold values from -0.1875 to 0.1875
Outputs:
- hidden_out: bfloat16 [64, 512, 768], P(('dp', 'fsdp'))
- raw_logits: bfloat16 [64, 12, 512, 512], P(('dp', 'fsdp'))
- grad_hidden: bfloat16 [64, 512, 768], P(('dp', 'fsdp'))
- grad_prev: bfloat16 [64, 12, 512, 512], P(('dp', 'fsdp'))
- grad_querymat: float32 [768, 768], P(('dp', 'fsdp'))
- grad_querybias: float32 [768], P(('dp', 'fsdp'))
- grad_keysmat: float32 [768, 768], P(('dp', 'fsdp'))
- grad_valuemat: float32 [768, 768], P(('dp', 'fsdp'))
- grad_valuebias: float32 [768], P(('dp', 'fsdp'))
- grad_outputmat: float32 [768, 768], P(('dp', 'fsdp'))
- grad_outputbias: float32 [768], P(('dp', 'fsdp'))
- grad_normgain: float32 [768], P(('dp', 'fsdp'))
- grad_normshift: float32 [768], P(('dp', 'fsdp'))
- grad_innermat: float32 [768, 3072], P(('dp', 'fsdp'))
- grad_innerbias: float32 [3072], P(('dp', 'fsdp'))
- grad_outermat: float32 [3072, 768], P(('dp', 'fsdp'))
- grad_outerbias: float32 [768], P(('dp', 'fsdp'))
- grad_lastgain: float32 [768], P(('dp', 'fsdp'))
- grad_lastshift: float32 [768], P(('dp', 'fsdp'))
The draws below stay inside these ranges and needn't reach their ends.
Inputs may be any that keep to these rules, and one draw needn't show every extreme that they name: In each slot the document numbers of real positions start at 0 and never fall; positions after a slot's last real one carry 512; slot j belongs to device j // 2.
All inputs are finite; a program needn't handle non-finite values.
Results may differ from the reference program's by a relative error of at most 0.013.
The reference program's roundings to bfloat16 on the way count: a program that leaves them out, or rounds other values in their place, can miss the bound.
Values may be sent and summed in bfloat16 or wider, within the bound.
No kernel may reach another device: no remote copies, remote signals or barrier semaphores. Data moves between devices by JAX's collectives and lax.ppermute only.
A program may use at most 256 MiB of HBM per device.

```python
import jax
import jax.numpy as jnp
from jax import lax

D = 768
H = 12
HD = 64
FF = 3072
S = 512
SLOT_DEV = 2
SLOTS = 64


def draw_document(key, part):
    first_key, second_key = jax.random.split(key)
    device_count = SLOTS // SLOT_DEV
    quarter = S // 4
    used_count = jax.random.randint(first_key, (device_count,), quarter, S + 1)
    used_count = used_count.at[0].set(S).at[1].set(quarter)
    per_slot = jnp.repeat(used_count, SLOT_DEV)
    position = jnp.arange(S)
    breaks = jax.random.randint(second_key, (SLOTS, S), 0, quarter) == 0
    whole_slot = (jnp.arange(SLOTS) % 4 == 0)[:, None]
    breaks = breaks & jnp.logical_not(whole_slot) & (position > 0)[None, :]
    doc_ids = jnp.cumsum(breaks.astype(jnp.int32), axis=1)
    return jnp.where(position[None, :] < per_slot[:, None], doc_ids, S).astype(jnp.int32)


def strengthened(values, key, source, target, shards_of, factor):
    def block_of(dim):
        return (jnp.arange(values.shape[dim]) // (values.shape[dim] // shards_of)).reshape((-1,) + (1,) * (values.ndim - 1 - dim))

    near = jax.random.permutation(key, shards_of)[block_of(target)]
    second = (block_of(target) + shards_of // 2) % shards_of
    return jnp.where((block_of(source) == near) | (block_of(source) == second), factor * values, values)


def level_of(key, extent, pieces, low, largest):
    gain = 1.0
    for axis_at, parts in pieces:
        draws = jax.random.uniform(jax.random.fold_in(jax.random.fold_in(key, 6), axis_at), (parts,), jnp.float32, low / len(pieces), largest / len(pieces))
        gain = gain * jnp.repeat(jnp.exp(draws), extent[axis_at] // parts).reshape((-1,) + (1,) * (len(extent) - 1 - axis_at))
    return gain


def scatter_about(own_key, dims, scale, limit, cuts=(), held_as=jnp.bfloat16):
    result = jax.random.normal(own_key, dims, jnp.float32) * scale
    if len(cuts) > 0:
        result = level_of(own_key, dims, cuts, -0.22, 0.18) * result
    return jnp.clip(result, min=-limit, max=limit).astype(held_as)


def gaussian_with(stream_key, shape, scale, reach, cuts, heavy, kind=jnp.bfloat16):
    values = scale * jax.random.normal(stream_key, shape, jnp.float32)
    if cuts:
        values = values * level_of(stream_key, shape, cuts, -0.22, 0.18)
    return jnp.clip(strengthened(values, jax.random.fold_in(stream_key, 3), *heavy), -reach, reach).astype(kind)


def setup_inputs(seed: int = 0) -> dict:
    seeds = jax.random.split(jax.random.key(seed), 21)
    return {
        "hidden_in": gaussian_with(seeds[0], (SLOTS, S, D), 1.0, 12.0, ((0, 32),), (0, 2, 32, 2.75)),
        "prev_logits": scatter_about(seeds[1], (SLOTS, H, S, S), 1.0, 6.0, ((0, 32),)),
        "document": draw_document(jax.random.fold_in(seeds[20], 71), 0),
        "querymat": scatter_about(seeds[3], (D, D), D ** -0.5, 0.21875, ((0, 32),)),
        "querybias": scatter_about(seeds[4], (D,), 0.3, 1.75, ((0, 32),)),
        "keysmat": scatter_about(seeds[5], (D, D), D ** -0.5, 0.21875, ((0, 32),)),
        "valuemat": scatter_about(seeds[6], (D, D), D ** -0.5, 0.21875, ((0, 32),)),
        "valuebias": scatter_about(seeds[7], (D,), 0.3, 1.75, ((0, 32),)),
        "outputmat": scatter_about(seeds[8], (D, D), (D // 16) ** -0.5, 0.875, ((0, 32),)),
        "outputbias": scatter_about(seeds[9], (D,), 0.3, 1.75, ((0, 32),)),
        "normgain": jnp.clip(1.0 + 0.1 * jax.random.normal(seeds[10], (D,), jnp.float32), 0.5, 1.5).astype(jnp.bfloat16),
        "normshift": scatter_about(seeds[11], (D,), 0.3, 1.75, ((0, 32),)),
        "innermat": scatter_about(seeds[12], (D, FF), D ** -0.5, 0.21875, ((0, 32),)),
        "innerbias": scatter_about(seeds[13], (FF,), 0.3, 1.75, ((0, 32),)),
        "outermat": scatter_about(seeds[14], (FF, D), FF ** -0.5, 0.109375, ((0, 32),)),
        "outerbias": scatter_about(seeds[15], (D,), 0.3, 1.75, ((0, 32),)),
        "lastgain": jnp.clip(1.0 + 0.1 * jax.random.normal(seeds[16], (D,), jnp.float32), 0.5, 1.5).astype(jnp.bfloat16),
        "lastshift": scatter_about(seeds[17], (D,), 0.3, 1.75, ((0, 32),)),
        "cotangent": scatter_about(seeds[18], (SLOTS, S, D), 1.0, 6.0, ((0, 32),)),
        "logit_cotangent": scatter_about(seeds[19], (SLOTS, H, S, S), 0.03, 0.1875, ((0, 32),)),
    }


@jax.custom_vjp
def low(v):
    return lax.optimization_barrier(v.astype(jnp.bfloat16)).astype(jnp.float32)

@jax.custom_vjp
def low_back(v):
    return v

def low_keep(v):
    return (low(v), None)

def low_pass(kept, grad):
    return (grad,)

def back_keep(v):
    return (v, None)

def back_low(kept, grad):
    return (low(grad),)
low.defvjp(low_keep, low_pass)
low_back.defvjp(back_keep, back_low)
NEGATIVE = -1e+30

def matmul(left, right):
    return jnp.dot(left, right, precision=lax.Precision.HIGHEST)

def layer_norm(values, norm_gain, norm_shift):
    average = lax.optimization_barrier(jnp.mean(values, -1, keepdims=True))
    centered = values - average
    spread = lax.optimization_barrier(jnp.mean(centered * centered, -1, keepdims=True))
    return centered * lax.rsqrt(spread + 1e-05) * norm_gain + norm_shift

def slot_forward(params, hidden, previous, doc_ids):
    querymat, querybias, keysmat, valuemat, valuebias, outputmat, outputbias, normgain, normshift, innermat, innerbias, outermat, outerbias, lastgain, lastshift = params
    factor = HD ** (-0.5)
    queries = low_back(low(matmul(hidden, querymat) + querybias)).reshape(S, H, HD)
    keysall = low_back(low(matmul(hidden, keysmat))).reshape(S, H, HD)
    values_all = low_back(low(matmul(hidden, valuemat) + valuebias)).reshape(S, H, HD)
    scores = jnp.einsum('qhd,khd->hqk', queries, keysall, precision=lax.Precision.HIGHEST) * factor + previous
    scores = low_back(scores)
    same_doc = doc_ids[:, None] == doc_ids[None, :]
    valid_rows = doc_ids < S
    paired = same_doc & valid_rows[:, None]
    logits_kept = jnp.where(paired[None], scores, 0.0)
    masked = jnp.where(same_doc[None], scores, NEGATIVE)
    attn_probs = jax.nn.softmax(masked, axis=-1)
    context = jnp.einsum('hqk,khd->qhd', low(attn_probs), values_all, precision=lax.Precision.HIGHEST)
    context = low_back(low(context.reshape(S, D)))
    attended = low_back(matmul(context, outputmat) + outputbias)
    first_norm = layer_norm(hidden + attended, normgain, normshift)
    inner_pre = low_back(matmul(low(first_norm), innermat) + innerbias)
    activated = low(jax.nn.gelu(inner_pre, approximate=False))
    outer_out = low_back(matmul(activated, outermat) + outerbias)
    final_norm = layer_norm(first_norm + outer_out, lastgain, lastshift)
    return (final_norm * valid_rows[:, None].astype(final_norm.dtype), logits_kept)

def reference(hidden_in, prev_logits, document, querymat, querybias, keysmat, valuemat, valuebias, outputmat, outputbias, normgain, normshift, innermat, innerbias, outermat, outerbias, lastgain, lastshift, cotangent, logit_cotangent):
    params = tuple((member.astype(jnp.float32) for member in (querymat, querybias, keysmat, valuemat, valuebias, outputmat, outputbias, normgain, normshift, innermat, innerbias, outermat, outerbias, lastgain, lastshift)))

    def one_slot(carry, slot_data):
        hidden, previous, doc_ids, grad_out, grad_logit = slot_data

        def forward(weights, hidden_full, previous_full):
            return slot_forward(weights, hidden_full, previous_full, doc_ids)
        outputs, pullback = jax.vjp(forward, params, hidden.astype(jnp.float32), previous.astype(jnp.float32))
        grads_params, grad_input, grad_previous = pullback((grad_out.astype(jnp.float32), grad_logit.astype(jnp.float32)))
        carry = jax.tree.map(jnp.add, carry, grads_params)
        return (carry, (outputs[0].astype(jnp.bfloat16), outputs[1].astype(jnp.bfloat16), grad_input.astype(jnp.bfloat16), grad_previous.astype(jnp.bfloat16)))
    zero_grads = tuple((jnp.zeros_like(member) for member in params))
    totals, stacked = lax.scan(one_slot, zero_grads, (hidden_in, prev_logits, document, cotangent, logit_cotangent))
    return (stacked[0], stacked[1], stacked[2], stacked[3], totals[0], totals[1], totals[2], totals[3], totals[4], totals[5], totals[6], totals[7], totals[8], totals[9], totals[10], totals[11], totals[12], totals[13], totals[14])
```

```python
from functools import partial

import jax
import jax.numpy as jnp
from jax import lax
from jax.experimental import pallas as pl
from jax.experimental.pallas import tpu as pltpu
from jax.sharding import PartitionSpec as P

NEGATIVE = -1e30
BF16 = jnp.bfloat16
F32 = jnp.float32


class Links:
    def __init__(self, dp_size, fsdp_size):
        self.dp_size = dp_size
        self.fsdp_size = fsdp_size
        self.line = fsdp_size // 2
        dp_at = lax.axis_index("dp")
        fsdp_at = lax.axis_index("fsdp")
        self.me = dp_at * fsdp_size + fsdp_at
        self.x = dp_at // 2
        self.core = dp_at % 2
        self.z = fsdp_at // 2
        self.y = fsdp_at % 2

    def over_core(self, value):
        return lax.ppermute(value, "dp", [(i, i ^ 1) for i in range(self.dp_size)])

    def over_x(self, value):
        return lax.ppermute(value, "dp", [(i, i ^ 2) for i in range(self.dp_size)])

    def over_y(self, value):
        return lax.ppermute(value, "fsdp", [(i, i ^ 1) for i in range(self.fsdp_size)])

    def to_right(self, value):
        return lax.ppermute(value, "fsdp", [(i, i + 2) for i in range(self.fsdp_size - 2)])

    def to_left(self, value):
        return lax.ppermute(value, "fsdp", [(i + 2, i) for i in range(self.fsdp_size - 2)])

    def owners(self, half):
        step = jnp.arange(8 * self.line, dtype=jnp.int32)
        line = step % self.line
        inner = (step // self.line) % 2
        outer = (step // (2 * self.line)) % 2
        x_bit, y_bit = (outer, inner) if half == 0 else (inner, outer)
        dp_at = (self.x ^ x_bit) * 2 + (self.core ^ (step // (4 * self.line)))
        return dp_at * self.fsdp_size + line * 2 + (self.y ^ y_bit)

    def positions(self, half):
        owner = jnp.arange(8 * self.line, dtype=jnp.int32)
        dp_at, fsdp_at = owner // self.fsdp_size, owner % self.fsdp_size
        x_bit, y_bit = (dp_at // 2) ^ self.x, (fsdp_at % 2) ^ self.y
        outer, inner = (x_bit, y_bit) if half == 0 else (y_bit, x_bit)
        core_bit = (dp_at % 2) ^ self.core
        return ((core_bit * 2 + outer) * 2 + inner) * self.line + fsdp_at // 2


def gather_line(links, own):
    pieces = [own]
    from_left = from_right = own
    for _ in range(links.line - 1):
        from_left = links.to_right(from_left)
        from_right = links.to_left(from_right)
        pieces = [from_left] + pieces + [from_right]
    return lax.dynamic_slice_in_dim(jnp.stack(pieces), links.line - 1 - links.z, links.line, 0)


def gather_halves(links, rows_a, rows_b):
    line = gather_line(links, jnp.concatenate([rows_a, rows_b], 0))
    half_a = line[:, : rows_a.shape[0]]
    half_b = line[:, rows_a.shape[0] :]
    pair_a = jnp.stack([half_a, links.over_y(half_a)])
    pair_b = jnp.stack([half_b, links.over_x(half_b)])
    far_a = links.over_x(pair_a)
    far_b = links.over_y(pair_b)
    core_a = links.over_core(pair_a)
    core_b = links.over_core(pair_b)
    return (
        (pair_a, far_a, core_a, links.over_core(far_a)),
        (pair_b, far_b, core_b, links.over_core(far_b)),
    )


def add_low(left, right):
    return (left.astype(F32) + right.astype(F32)).astype(BF16)


def scatter_line(links, blocks):
    count = links.line
    right = left = None
    for hop in range(1, count):
        send_right = lax.dynamic_index_in_dim(
            blocks, jnp.minimum(links.z + count - hop, count - 1), 0, keepdims=False
        )
        send_left = lax.dynamic_index_in_dim(
            blocks, jnp.maximum(links.z - count + hop, 0), 0, keepdims=False
        )
        if right is not None:
            send_right = add_low(send_right, right)
            send_left = add_low(send_left, left)
        right = links.to_right(send_right)
        left = links.to_left(send_left)
    own = lax.dynamic_index_in_dim(blocks, links.z, 0, keepdims=False).astype(F32)
    return own + right.astype(F32) + left.astype(F32)


def scatter_half(links, near, far, first, second):
    arrived = links.over_core(far)
    keep = add_low(near[0], arrived[0])
    send = add_low(near[1], arrived[1])
    arrived = first(send)
    kept = add_low(keep[0], arrived[0])
    send = add_low(keep[1], arrived[1])
    return scatter_line(links, add_low(kept, second(send)))


def clipped(line, phase):
    def at(step, owners):
        inside = jnp.clip(step - phase * 2 * line, 0, 2 * line - 1)
        return (inside // line, inside % line, 0, 0)

    return at


def unpack_kernel(layout, sums, span, owners, *refs):
    sources, outs = refs[:4], refs[4:]
    phase = pl.program_id(0) // span
    if sums:

        @pl.when(pl.program_id(0) == 0)
        def _():
            outs[-1][...] = jnp.zeros_like(outs[-1])

    for number, source in enumerate(sources):

        @pl.when(phase == number)
        def _():
            at = 0
            for (rows, blocks), out in zip(layout, outs):
                width = out.shape[1] // blocks
                for block in range(blocks):
                    out[:, block * width : (block + 1) * width] = source[at : at + rows, :]
                    at += rows
            if sums:
                outs[-1][...] += source[at:, :].astype(F32)


def unpack(links, half, arrays, layout, sums):
    line, rows, width = arrays[0].shape[1:]
    count = 8 * line
    if any(part[0] % 8 for part in layout):
        whole = jnp.concatenate([a.reshape(2 * line, rows, width) for a in arrays], 0)
        whole = jnp.take(whole, links.positions(half), axis=0)
        outs, at = [], 0
        for part_rows, blocks in layout:
            piece = whole[:, at : at + part_rows * blocks].reshape(count, blocks, part_rows, width)
            outs.append(piece.transpose(0, 2, 1, 3).reshape(count * part_rows, blocks * width))
            at += part_rows * blocks
        if sums:
            outs.append(jnp.sum(whole[:, at:].astype(F32), 0))
        return outs
    out_shape = [jax.ShapeDtypeStruct((count * r, b * width), BF16) for r, b in layout]
    out_specs = [pl.BlockSpec((r, b * width), lambda step, owners: (owners[step], 0)) for r, b in layout]
    if sums:
        out_shape.append(jax.ShapeDtypeStruct((sums, width), F32))
        out_specs.append(pl.BlockSpec((sums, width), lambda step, owners: (0, 0)))
    return pl.pallas_call(
        partial(unpack_kernel, layout, sums, 2 * line),
        grid_spec=pltpu.PrefetchScalarGridSpec(
            num_scalar_prefetch=1,
            grid=(count,),
            in_specs=[
                pl.BlockSpec((None, None, rows, width), clipped(line, phase)) for phase in range(4)
            ],
            out_specs=out_specs,
        ),
        out_shape=out_shape,
        cost_estimate=pl.CostEstimate(
            flops=0, bytes_accessed=4 * count * rows * width, transcendentals=0
        ),
        name="unpack",
    )(links.owners(half), *arrays)


def clipped_pair(line, phase):
    def at(step, owners):
        inside = jnp.clip(step - phase * 4 * line, 0, 4 * line - 1)
        return (inside // (2 * line), (inside // line) % 2, inside % line, 0, 0)

    return at


def pack_kernel(layout, sums, span, owners, *refs):
    parts, outs = refs[:-2], refs[-2:]
    phase = pl.program_id(0) // span
    for number, out in enumerate(outs):

        @pl.when(phase == number)
        def _():
            at = 0
            for (rows, blocks), part in zip(layout, parts):
                width = part.shape[1] // blocks
                for block in range(blocks):
                    out[at : at + rows, :] = part[:, block * width : (block + 1) * width].astype(BF16)
                    at += rows
            if sums:
                out[at:, :] = parts[-1][...].astype(BF16)


def pack(links, half, parts, layout, sums):
    line = links.line
    count = 8 * line
    rows = sum(r * b for r, b in layout) + sums
    width = parts[0].shape[1] // layout[0][1]
    if any(part[0] % 8 for part in layout):
        pieces = [
            part.reshape(count, r, b, width).transpose(0, 2, 1, 3).reshape(count, r * b, width)
            for part, (r, b) in zip(parts, layout)
        ]
        if sums:
            pieces.append(jnp.broadcast_to(parts[-1][None], (count, sums, width)))
        whole = jnp.concatenate(pieces, 1).astype(BF16)
        whole = jnp.take(whole, links.owners(half), axis=0).reshape(2, 2, 2, line, rows, width)
        return whole[0], whole[1]
    in_specs = [pl.BlockSpec((r, b * width), lambda step, owners: (owners[step], 0)) for r, b in layout]
    if sums:
        in_specs.append(pl.BlockSpec((sums, width), lambda step, owners: (0, 0)))
    shape = jax.ShapeDtypeStruct((2, 2, line, rows, width), BF16)
    return pl.pallas_call(
        partial(pack_kernel, layout, sums, 4 * line),
        grid_spec=pltpu.PrefetchScalarGridSpec(
            num_scalar_prefetch=1,
            grid=(count,),
            in_specs=in_specs,
            out_specs=[
                pl.BlockSpec((None, None, None, rows, width), clipped_pair(line, phase))
                for phase in range(2)
            ],
        ),
        out_shape=[shape, shape],
        cost_estimate=pl.CostEstimate(
            flops=0, bytes_accessed=6 * count * rows * width, transcendentals=0
        ),
        name="pack",
    )(links.owners(half), *parts)


def stacked(shard, width):
    rows = shard.shape[0]
    blocks = shard.shape[1] // width
    return jnp.concatenate([shard[:, i * width : (i + 1) * width] for i in range(blocks)], 0)


VECTORS = 16


def vector_rows(links, vectors, width):
    count = 8 * links.line
    rows = []
    for shard in vectors:
        size = shard.shape[0]
        spot = jnp.arange(count, dtype=jnp.int32)[:, None] == links.me
        rows.append(jnp.where(spot, shard[None], jnp.zeros_like(shard)[None]).reshape(-1, width))
    rows = jnp.concatenate(rows, 0)
    return jnp.pad(rows, ((0, VECTORS - rows.shape[0]), (0, 0)))


def layer_norm(values, norm_gain, norm_shift):
    average = jnp.mean(values, -1, keepdims=True)
    centered = values - average
    spread = jnp.mean(centered * centered, -1, keepdims=True)
    scaled = lax.rsqrt(spread + 1e-05)
    normal = centered * scaled
    return (normal * norm_gain + norm_shift, normal, scaled)


def norm_back(grad_in, normal, scaled, norm_gain):
    weighted = grad_in * norm_gain
    grad_gain = jnp.sum(grad_in * normal, 0)
    grad_shift = jnp.sum(grad_in, 0)
    centered = weighted - jnp.mean(weighted, -1, keepdims=True)
    grad_values = scaled * (centered - normal * jnp.mean(weighted * normal, -1, keepdims=True))
    return (grad_values, grad_gain, grad_shift)


def split_heads(tensor, slot_count, head_count):
    total_rows, model_width = tensor.shape
    length = total_rows // slot_count
    return tensor.reshape(slot_count, length, head_count, model_width // head_count)


def slot_scores(query_h, key_h, previous, doc_ids, factor):
    scores = jnp.einsum("qhd,khd->hqk", query_h, key_h, preferred_element_type=jnp.float32) * factor
    scores = scores + previous.astype(jnp.float32)
    same_doc = doc_ids[:, None] == doc_ids[None, :]
    paired = same_doc & (doc_ids < doc_ids.shape[0])[:, None]
    masked = jnp.where(same_doc[None], scores, NEGATIVE)
    return (scores, masked, paired)


def forward_pass(weights, flat_in, prev_logits, document, valid_rows, factor):
    (
        querymat,
        querybias,
        keysmat,
        valuemat,
        valuebias,
        outputmat,
        outputbias,
        normgain,
        normshift,
        innermat,
        innerbias,
        outermat,
        outerbias,
        lastgain,
        lastshift,
    ) = weights
    slot_count, length = document.shape
    head_count = prev_logits.shape[1]
    total_rows, model_width = flat_in.shape
    queries = (
        jnp.dot(flat_in, querymat, preferred_element_type=jnp.float32)
        + querybias.astype(jnp.float32)
    ).astype(jnp.bfloat16)
    keysall = jnp.dot(flat_in, keysmat, preferred_element_type=jnp.float32).astype(jnp.bfloat16)
    values_all = (
        jnp.dot(flat_in, valuemat, preferred_element_type=jnp.float32)
        + valuebias.astype(jnp.float32)
    ).astype(jnp.bfloat16)

    def attend(pieces):
        query_h, key_h, value_h, previous, doc_ids = pieces
        scores, masked, paired = slot_scores(query_h, key_h, previous, doc_ids, factor)
        logits_out = jnp.where(paired[None], scores, 0.0).astype(jnp.bfloat16)
        row_max = jnp.max(masked, -1, keepdims=True)
        exponent = jnp.exp(masked - row_max)
        exp_total = jnp.sum(exponent, -1, keepdims=True)
        attn_probs = exponent / exp_total
        logsum = row_max + jnp.log(exp_total)
        context = jnp.einsum(
            "hqk,khd->qhd",
            attn_probs.astype(jnp.bfloat16),
            value_h,
            preferred_element_type=jnp.float32,
        ).astype(jnp.bfloat16)
        return (logits_out, context.reshape(length, model_width), logsum)

    raw_logits, context, logsums = lax.map(
        attend,
        (
            split_heads(queries, slot_count, head_count),
            split_heads(keysall, slot_count, head_count),
            split_heads(values_all, slot_count, head_count),
            prev_logits,
            document,
        ),
    )
    context = context.reshape(total_rows, model_width)
    attended = jnp.dot(context, outputmat, preferred_element_type=jnp.float32) + outputbias.astype(
        jnp.float32
    )
    first_norm, normal_one, scale_one = layer_norm(
        flat_in.astype(jnp.float32) + attended,
        normgain.astype(jnp.float32),
        normshift.astype(jnp.float32),
    )
    first_low = first_norm.astype(jnp.bfloat16)
    inner_pre = jnp.dot(first_low, innermat, preferred_element_type=jnp.float32) + innerbias.astype(
        jnp.float32
    )
    activated = jax.nn.gelu(inner_pre, approximate=False).astype(jnp.bfloat16)
    outer_out = jnp.dot(activated, outermat, preferred_element_type=jnp.float32) + outerbias.astype(
        jnp.float32
    )
    final_norm, normal_two, scale_two = layer_norm(
        first_norm + outer_out, lastgain.astype(jnp.float32), lastshift.astype(jnp.float32)
    )
    hidden_out = (
        (final_norm * valid_rows).astype(jnp.bfloat16).reshape(slot_count, length, model_width)
    )
    kept_state = (
        queries,
        keysall,
        values_all,
        logsums,
        context,
        normal_one,
        scale_one,
        first_low,
        inner_pre,
        activated,
        normal_two,
        scale_two,
    )
    return ((hidden_out, raw_logits), kept_state)


def body(
    hidden_in,
    prev_logits,
    document,
    querymat,
    querybias,
    keysmat,
    valuemat,
    valuebias,
    outputmat,
    outputbias,
    normgain,
    normshift,
    innermat,
    innerbias,
    outermat,
    outerbias,
    lastgain,
    lastshift,
    cotangent,
    logit_cotangent,
):
    slot_count, length, model_width = hidden_in.shape
    head_count = prev_logits.shape[1]
    total_rows = slot_count * length
    factor = (model_width // head_count) ** (-0.5)
    flat_in = hidden_in.reshape(total_rows, model_width)
    valid_rows = (document < length).reshape(total_rows, 1).astype(jnp.float32)
    links = Links(lax.axis_size("dp"), lax.axis_size("fsdp"))
    low_rows = querymat.shape[0]
    wide = innermat.shape[1] // model_width
    vectors = (querybias, valuebias, outputbias, normgain, normshift, outerbias, lastgain, lastshift, innerbias)
    layout_qk = ((low_rows, 1), (low_rows, 1))
    layout_v = ((low_rows, 1),)
    layout_oi = ((low_rows, 1), (low_rows, wide))
    layout_outer = ((outermat.shape[0], 1),)
    gathered_qk, gathered_v = gather_halves(
        links,
        jnp.concatenate([querymat, keysmat], 0),
        jnp.concatenate([valuemat, vector_rows(links, vectors, model_width)], 0),
    )
    gathered_oi, gathered_outer = gather_halves(
        links, jnp.concatenate([outputmat, stacked(innermat, model_width)], 0), outermat
    )
    full_query, full_keys = unpack(links, 0, gathered_qk, layout_qk, 0)
    full_value, whole_vectors = unpack(links, 1, gathered_v, layout_v, VECTORS)
    full_output, full_inner = unpack(links, 0, gathered_oi, layout_oi, 0)
    (full_outer,) = unpack(links, 1, gathered_outer, layout_outer, 0)
    full_qbias, full_vbias, full_obias, full_normgain, full_normshift, full_obias2, full_lastgain, full_lastshift = (
        whole_vectors[i] for i in range(8)
    )
    full_ibias = whole_vectors[8 : 8 + wide].reshape(-1)
    gathered = (
        full_query, full_qbias, full_keys, full_value, full_vbias, full_output, full_obias, full_normgain,
        full_normshift, full_inner, full_ibias, full_outer, full_obias2, full_lastgain, full_lastshift,
    )
    layer_out, kept_state = forward_pass(
        gathered, flat_in, prev_logits, document, valid_rows, factor
    )
    (
        queries,
        keysall,
        values_all,
        logsums,
        context,
        normal_one,
        scale_one,
        first_low,
        inner_pre,
        activated,
        normal_two,
        scale_two,
    ) = kept_state
    grad_last = cotangent.reshape(total_rows, model_width).astype(jnp.float32) * valid_rows
    grad_sum2, grad_lastgain, grad_lastshift = norm_back(
        grad_last, normal_two, scale_two, full_lastgain.astype(jnp.float32)
    )
    grad_outer = grad_sum2.astype(jnp.bfloat16)
    grad_outermat = jnp.einsum(
        "rf,rd->fd", activated, grad_outer, preferred_element_type=jnp.float32
    )
    grad_outerbias = jnp.sum(grad_outer.astype(jnp.float32), 0)
    grad_activated = jnp.einsum(
        "rd,fd->rf", grad_outer, full_outer, preferred_element_type=jnp.float32
    )
    unused_value, gelu_back = jax.vjp(partial(jax.nn.gelu, approximate=False), inner_pre)
    grad_inner = gelu_back(grad_activated)[0].astype(jnp.bfloat16)
    grad_innermat = jnp.einsum(
        "rd,rf->df", first_low, grad_inner, preferred_element_type=jnp.float32
    )
    grad_innerbias = jnp.sum(grad_inner.astype(jnp.float32), 0)
    grad_first = grad_sum2 + jnp.einsum(
        "rf,df->rd", grad_inner, full_inner, preferred_element_type=jnp.float32
    )
    grad_sum1, grad_normgain, grad_normshift = norm_back(
        grad_first, normal_one, scale_one, full_normgain.astype(jnp.float32)
    )
    grad_attended = grad_sum1.astype(jnp.bfloat16)
    grad_outputmat = jnp.einsum(
        "rc,rd->cd", context, grad_attended, preferred_element_type=jnp.float32
    )
    grad_outputbias = jnp.sum(grad_attended.astype(jnp.float32), 0)
    grad_context = jnp.einsum(
        "rd,cd->rc", grad_attended, full_output, preferred_element_type=jnp.float32
    ).astype(jnp.bfloat16)

    def attend_back(pieces):
        query_h, key_h, value_h, previous, doc_ids, logsum, grad_ctx, grad_logit = pieces
        scores, masked, paired = slot_scores(query_h, key_h, previous, doc_ids, factor)
        attn_probs = jnp.exp(masked - logsum)
        grad_probs = jnp.einsum(
            "qhd,khd->hqk", grad_ctx, value_h, preferred_element_type=jnp.float32
        )
        grad_value = jnp.einsum(
            "hqk,qhd->khd",
            attn_probs.astype(jnp.bfloat16),
            grad_ctx,
            preferred_element_type=jnp.float32,
        )
        inner_sum = jnp.sum(attn_probs * grad_probs, -1, keepdims=True)
        grad_scores = attn_probs * (grad_probs - inner_sum)
        grad_scores = (
            grad_scores + jnp.where(paired[None], grad_logit.astype(jnp.float32), 0.0)
        ).astype(jnp.bfloat16)
        grad_query = (
            jnp.einsum("hqk,khd->qhd", grad_scores, key_h, preferred_element_type=jnp.float32)
            * factor
        )
        grad_key = (
            jnp.einsum("hqk,qhd->khd", grad_scores, query_h, preferred_element_type=jnp.float32)
            * factor
        )
        return (
            grad_scores,
            grad_query.astype(jnp.bfloat16).reshape(length, model_width),
            grad_key.astype(jnp.bfloat16).reshape(length, model_width),
            grad_value.astype(jnp.bfloat16).reshape(length, model_width),
        )

    grad_prev, grad_queries, grad_keys, grad_values = lax.map(
        attend_back,
        (
            split_heads(queries, slot_count, head_count),
            split_heads(keysall, slot_count, head_count),
            split_heads(values_all, slot_count, head_count),
            prev_logits,
            document,
            logsums,
            split_heads(grad_context, slot_count, head_count),
            logit_cotangent,
        ),
    )
    grad_queries = grad_queries.reshape(total_rows, model_width)
    grad_keys = grad_keys.reshape(total_rows, model_width)
    grad_values = grad_values.reshape(total_rows, model_width)
    grad_querymat = jnp.einsum(
        "rd,re->de", flat_in, grad_queries, preferred_element_type=jnp.float32
    )
    grad_querybias = jnp.sum(grad_queries.astype(jnp.float32), 0)
    grad_keysmat = jnp.einsum("rd,re->de", flat_in, grad_keys, preferred_element_type=jnp.float32)
    grad_valuemat = jnp.einsum(
        "rd,re->de", flat_in, grad_values, preferred_element_type=jnp.float32
    )
    grad_valuebias = jnp.sum(grad_values.astype(jnp.float32), 0)
    grad_input = grad_sum1 + jnp.einsum(
        "re,de->rd", grad_queries, full_query, preferred_element_type=jnp.float32
    )
    grad_input = grad_input + jnp.einsum(
        "re,de->rd", grad_keys, full_keys, preferred_element_type=jnp.float32
    )
    grad_input = grad_input + jnp.einsum(
        "re,de->rd", grad_values, full_value, preferred_element_type=jnp.float32
    )
    grad_hidden = grad_input.astype(jnp.bfloat16).reshape(slot_count, length, model_width)
    near_oi, far_oi = pack(links, 0, (grad_outputmat, grad_innermat), layout_oi, 0)
    near_outer, far_outer = pack(links, 1, (grad_outermat,), layout_outer, 0)
    vector_grads = jnp.concatenate(
        [
            grad_querybias, grad_valuebias, grad_outputbias, grad_normgain, grad_normshift, grad_outerbias,
            grad_lastgain, grad_lastshift, grad_innerbias,
        ]
    ).reshape(-1, model_width)
    vector_grads = jnp.pad(vector_grads, ((0, VECTORS - vector_grads.shape[0]), (0, 0)))
    near_qk, far_qk = pack(links, 0, (grad_querymat, grad_keysmat), layout_qk, 0)
    near_v, far_v = pack(links, 1, (grad_valuemat, vector_grads), layout_v, VECTORS)
    own_oi = scatter_half(links, near_oi, far_oi, links.over_x, links.over_y)
    own_outer = scatter_half(links, near_outer, far_outer, links.over_y, links.over_x)
    own_qk = scatter_half(links, near_qk, far_qk, links.over_x, links.over_y)
    own_v = scatter_half(links, near_v, far_v, links.over_y, links.over_x)
    own_vectors = own_v[low_rows:]

    def own_vector(row):
        return lax.dynamic_slice_in_dim(own_vectors[row], links.me * low_rows, low_rows, 0)

    own_inner = jnp.concatenate(
        [own_oi[low_rows * (i + 1) : low_rows * (i + 2)] for i in range(wide)], 1
    )
    own_ibias = lax.dynamic_slice_in_dim(
        own_vectors[8 : 8 + wide].reshape(-1), links.me * wide * low_rows, wide * low_rows, 0
    )
    owned = (
        own_qk[:low_rows], own_vector(0), own_qk[low_rows:], own_v[:low_rows], own_vector(1),
        own_oi[:low_rows], own_vector(2), own_vector(3), own_vector(4), own_inner, own_ibias,
        own_outer, own_vector(5), own_vector(6), own_vector(7),
    )
    return (layer_out[0], layer_out[1], grad_hidden, grad_prev) + owned


def solution(mesh):
    placed = (
        P(("dp", "fsdp"), None, None),
        P(("dp", "fsdp"), None, None, None),
        P(("dp", "fsdp"), None),
        P(("dp", "fsdp"), None),
        P(("dp", "fsdp")),
        P(("dp", "fsdp"), None),
        P(("dp", "fsdp"), None),
        P(("dp", "fsdp")),
        P(("dp", "fsdp"), None),
        P(("dp", "fsdp")),
        P(("dp", "fsdp")),
        P(("dp", "fsdp")),
        P(("dp", "fsdp"), None),
        P(("dp", "fsdp")),
        P(("dp", "fsdp"), None),
        P(("dp", "fsdp")),
        P(("dp", "fsdp")),
        P(("dp", "fsdp")),
        P(("dp", "fsdp"), None, None),
        P(("dp", "fsdp"), None, None, None),
    )
    return jax.shard_map(
        body,
        mesh=mesh,
        in_specs=placed,
        out_specs=(
            P(("dp", "fsdp"), None, None),
            P(("dp", "fsdp"), None, None, None),
            P(("dp", "fsdp"), None, None),
            P(("dp", "fsdp"), None, None, None),
            P(("dp", "fsdp"), None),
            P(("dp", "fsdp")),
            P(("dp", "fsdp"), None),
            P(("dp", "fsdp"), None),
            P(("dp", "fsdp")),
            P(("dp", "fsdp"), None),
            P(("dp", "fsdp")),
            P(("dp", "fsdp")),
            P(("dp", "fsdp")),
            P(("dp", "fsdp"), None),
            P(("dp", "fsdp")),
            P(("dp", "fsdp"), None),
            P(("dp", "fsdp")),
            P(("dp", "fsdp")),
            P(("dp", "fsdp")),
        ),
        check_vma=False,
    )
```
